32 devices in a mesh: chan: 16 (over z, y, x), tm: 2 (over core).
Axes of the slice: x: 2, y: 2, z: 4, core: 2. Of those that a mesh axis runs over, the one named last changes fastest.
Arguments:
- data: float32 [2560, 256], P('chan', 'tm'), may hold values from -40 to 40
- templates: float32 [32, 2048], P('tm'), may hold values from -6 to 6
Outputs:
- zscore: float32 [32, 2560, 256], P(None, 'chan', 'tm')
- detection: float32 [32, 256], P(None, 'tm')
- peak: float32 [32, 256], P(None, 'tm')
The draws below stay inside these ranges and needn't reach their ends.
All inputs are finite; a program needn't handle non-finite values.
Results may differ from the reference program's by a relative error of at most 0.00013.
Values sent between devices are 32-bit elements; how exact they have to be, the bound alone decides.
A program may use at most 192 MiB of HBM per device.

```python
import math
import jax
import jax.numpy as jnp
from jax import lax

K = 32
TC = 16
TL = 128
NCH = 2560
NT = 256
PATCH = 2048


def draw_data(key, part):
    base_key = jax.random.fold_in(key, 11)
    key_base, key_chan, key_time = jax.random.split(base_key, 3)
    chan_scale = jnp.exp(jax.random.uniform(key_chan, (NCH, 1), jnp.float32) * math.log(10.0))
    time_scale = jnp.exp(jax.random.uniform(key_time, (1, NT), jnp.float32) * math.log(10.0))
    base = jnp.clip(jax.random.normal(key_base, (NCH, NT), jnp.float32), -3.9, 3.9)
    return (base * chan_scale * time_scale / 10.0).astype(jnp.float32)


def block_scale(stream_key, extent, cuts, least, largest):
    def one(position, shards_of):
        draws = jax.random.uniform(jax.random.fold_in(jax.random.fold_in(stream_key, 6), position), (shards_of,), jnp.float32, least / len(cuts), largest / len(cuts))
        return jnp.repeat(jnp.exp(draws), extent[position] // shards_of).reshape((-1,) + (1,) * (len(extent) - position - 1))

    gain = one(*cuts[0])
    for cut in cuts[1:]:
        gain = gain * one(*cut)
    return gain


def scatter_about(own_key, shape, scale, limit, shards=(), held_as=jnp.bfloat16):
    level = block_scale(own_key, shape, shards, -0.22, 0.18) if shards else 1.0
    result = jax.random.normal(own_key, shape, jnp.float32) * scale * level
    return jnp.minimum(jnp.maximum(result, -limit), limit).astype(held_as)


def setup_inputs(seed: int = 0) -> dict:
    key_list = jax.random.split(jax.random.key(seed), 3)
    data = draw_data(jax.random.fold_in(key_list[2], 71), 0)
    templates = scatter_about(key_list[1], (K, PATCH), 1.0, 6.0, ((0, 2),), jnp.float32)
    return dict(data=data, templates=templates)


EPS = 1e-06

def hankel_rows(segment, width, lags):
    rows, span = segment.shape
    tiled = jnp.tile(segment, (1, width + 1))[:, :width * (span + 1)]
    return tiled.reshape(rows, width, span + 1)[:, :, :lags]

def reference(data, templates):
    extended = jnp.concatenate([data, data[:, :TL - 1]], axis=1)
    extended = jnp.concatenate([extended, jnp.zeros((TC - 1, extended.shape[1]), jnp.float32)], axis=0)
    squares = extended * extended
    chanwin = squares[0:NCH]
    for i in range(1, TC):
        chanwin = chanwin + squares[i:i + NCH]
    cumul = jnp.cumsum(jnp.concatenate([jnp.zeros((NCH, 1), jnp.float32), chanwin], axis=1), axis=1)
    energy = cumul[:, TL:TL + NT] - cumul[:, :NT]
    inverse = 1.0 / (jnp.sqrt(energy / PATCH + EPS) * math.sqrt(PATCH))
    spread = jnp.sqrt(lax.optimization_barrier(jnp.mean(templates * templates, axis=1)) + EPS)
    shaped = templates.reshape(K, TC, TL)
    width = math.gcd(NT, 32)
    count = NT // width

    def one_block(index):
        segment = lax.dynamic_slice_in_dim(extended, index * width, width + TL - 1, 1)
        hankel = hankel_rows(segment, width, TL)
        total = jnp.zeros((K, NCH * width), jnp.float32)
        for i in range(TC):
            window = hankel[i:i + NCH].reshape(NCH * width, TL)
            total = total + lax.dot_general(shaped[:, i, :], window, (((1,), (1,)), ((), ())), precision=lax.Precision.HIGHEST, preferred_element_type=jnp.float32)
        return total.reshape(K, NCH, width)
    blocks = lax.map(one_block, jnp.arange(count, dtype=jnp.int32))
    corr = jnp.transpose(blocks, (1, 2, 0, 3)).reshape(K, NCH, NT)
    zscore = corr * inverse[None, :, :] / spread[:, None, None]
    detection = lax.optimization_barrier(jnp.sum(zscore, axis=1)) / math.sqrt(NCH)
    peak = lax.optimization_barrier(jnp.max(zscore, axis=1))
    return (zscore, detection, peak)
```

```python
import functools
import math

import jax
import jax.numpy as jnp
from jax import lax
from jax.experimental import pallas as pl
from jax.experimental.pallas import tpu as pltpu
from jax.sharding import PartitionSpec as P

TC = 16
TL = 128
PATCH = 2048
EPS = 1e-06
W = 16
HEADS = TC * TL
DEPTH = HEADS + TC * W
CB = 32
MESH = pl.DeviceIdType.MESH


def exchange_kernel(nc, nt, data_ref, tmpl_ref, ext_ref, tall_ref, send, recv, tsend, trecv):
    rows = data_ref.shape[0]
    c = lax.axis_index("chan")
    t = lax.axis_index("tm")
    prev_t = lax.rem(t + nt - 1, nt)
    next_t = lax.rem(t + 1, nt)
    barrier = pltpu.get_barrier_semaphore()
    for d in range(1, nt):
        pl.semaphore_signal(barrier, inc=1, device_id=(c, lax.rem(t + d, nt)), device_id_type=MESH)

    @pl.when(c < nc - 1)
    def _():
        pl.semaphore_signal(barrier, inc=1, device_id=(c + 1, t), device_id_type=MESH)
        pl.semaphore_signal(barrier, inc=1, device_id=(c + 1, next_t), device_id_type=MESH)

    ext_ref[0, 0:rows, :] = data_ref[...]
    tall_ref[t] = tmpl_ref[...]

    @pl.when(c == nc - 1)
    def _():
        ext_ref[:, rows:, :] = jnp.zeros((2, TC, ext_ref.shape[2]), jnp.float32)

    @pl.when(c > 0)
    def _():
        pl.semaphore_wait(barrier, nt + 1)

    @pl.when(c == 0)
    def _():
        pl.semaphore_wait(barrier, nt - 1)

    def side(which, slot, device):
        return pltpu.make_async_remote_copy(
            src_ref=data_ref.at[pl.ds(0, TC)], dst_ref=ext_ref.at[which, pl.ds(rows, TC)],
            send_sem=send.at[slot], recv_sem=recv.at[slot],
            device_id=device, device_id_type=MESH)

    trail = pltpu.make_async_remote_copy(
        src_ref=data_ref, dst_ref=ext_ref.at[1, pl.ds(0, rows)],
        send_sem=send.at[0], recv_sem=recv.at[0],
        device_id=(c, prev_t), device_id_type=MESH)

    @pl.when(c > 0)
    def _():
        side(0, 1, (c - 1, t)).start()
        side(1, 2, (c - 1, prev_t)).start()

    every = []
    for d in range(1, nt):
        cp = pltpu.make_async_remote_copy(
            src_ref=tmpl_ref, dst_ref=tall_ref.at[t],
            send_sem=tsend.at[d - 1], recv_sem=trecv.at[d - 1],
            device_id=(c, lax.rem(t + d, nt)), device_id_type=MESH)
        cp.start()
        every.append(cp)
    trail.start()
    for cp in every:
        cp.wait()
    trail.wait()

    @pl.when(c > 0)
    def _():
        side(0, 1, (c - 1, t)).wait_send()
        side(1, 2, (c - 1, prev_t)).wait_send()

    @pl.when(c < nc - 1)
    def _():
        side(0, 1, (c, t)).wait_recv()
        side(1, 2, (c, t)).wait_recv()


def exchange(data, templates, nc, nt):
    rows, cols = data.shape
    kt = templates.shape[0]
    vmem = pl.BlockSpec(memory_space=pltpu.VMEM)
    return pl.pallas_call(
        functools.partial(exchange_kernel, nc, nt),
        out_shape=(
            jax.ShapeDtypeStruct((2, rows + TC, cols), jnp.float32),
            jax.ShapeDtypeStruct((nt, kt, PATCH), jnp.float32),
        ),
        in_specs=[vmem, vmem],
        out_specs=(vmem, vmem),
        scratch_shapes=[
            pltpu.SemaphoreType.DMA((3,)),
            pltpu.SemaphoreType.DMA((3,)),
            pltpu.SemaphoreType.DMA((max(nt - 1, 1),)),
            pltpu.SemaphoreType.DMA((max(nt - 1, 1),)),
        ],
        compiler_params=pltpu.CompilerParams(collective_id=0, has_side_effects=True),
    )(data, templates)


def split(x):
    hi = x.astype(jnp.bfloat16)
    lo = (x - hi.astype(jnp.float32)).astype(jnp.bfloat16)
    return hi, lo


def correlate_kernel(ext_ref, tmpl_ref, z_ref, sum_ref, max_ref,
                     whi, wlo, lhi, llo, tn, inv, f1, fhi, flo, acc, dsum, dmax):
    step = pl.program_id(0)
    count = tmpl_ref.shape[0]
    rows = inv.shape[0]
    nb = TL // W
    lane = lax.broadcasted_iota(jnp.int32, (W, TL), 1)
    sub = lax.broadcasted_iota(jnp.int32, (W, TL), 0)

    @pl.when(step == 0)
    def _():
        tmpl = tmpl_ref[...]
        spread = jnp.sqrt(jnp.sum(tmpl * tmpl, axis=1, keepdims=True) / PATCH + EPS)
        tn[...] = tmpl * (1.0 / spread)

        def eight_templates(kg, carry):
            k0 = pl.multiple_of(kg * 8, 8)
            for q in range(8):
                r0 = pl.multiple_of(kg * (8 * W) + q * W, W)
                tails = [jnp.zeros((W, TL), jnp.float32) for _ in range(2)]
                for i in range(TC):
                    row = tn[pl.ds(k0, 8), i * TL:(i + 1) * TL][q:q + 1]
                    row = jnp.broadcast_to(row, (W, TL))
                    rolled = pltpu.roll(row, 0, 1, stride=1, stride_axis=0)
                    hi, lo = split(jnp.where(lane >= sub, rolled, 0.0))
                    whi[pl.ds(r0, W), i * TL:(i + 1) * TL] = hi
                    wlo[pl.ds(r0, W), i * TL:(i + 1) * TL] = lo
                    tail = jnp.where(lane < sub, rolled, 0.0)
                    g, p = divmod(i, 8)
                    tails[g] = tails[g] + (pltpu.roll(tail, W * p, 1) if p else tail)
                for g in range(2):
                    hi, lo = split(tails[g])
                    whi[pl.ds(r0, W), HEADS + g * TL:HEADS + (g + 1) * TL] = hi
                    wlo[pl.ds(r0, W), HEADS + g * TL:HEADS + (g + 1) * TL] = lo
            return carry

        lax.fori_loop(0, count // 8, eight_templates, 0)
        pieces = []
        for h in range(2):
            sq = ext_ref[h] * ext_ref[h]
            s = sq[0:rows + 8] + sq[1:rows + 9]
            s = s[0:rows + 6] + s[2:rows + 8]
            s = s[0:rows + 2] + s[4:rows + 6]
            e = sq[8:rows + TC]
            s_low = s[0:rows]
            u = e[0:rows + 7] + e[1:rows + 8]
            u = u[0:rows + 5] + u[2:rows + 7]
            u = u[0:rows] + u[4:rows + 4]
            pieces.append(s_low + u)
        win = jnp.concatenate(pieces, axis=1)
        src = lax.broadcasted_iota(jnp.int32, (2 * TL, TL), 0)
        dst = lax.broadcasted_iota(jnp.int32, (2 * TL, TL), 1)
        band = jnp.where((src >= dst) & (src < dst + TL), 1.0, 0.0).astype(jnp.bfloat16)
        energy = jnp.zeros((rows, TL), jnp.float32)
        rest = win
        for _ in range(3):
            part = rest.astype(jnp.bfloat16)
            rest = rest - part.astype(jnp.float32)
            energy = energy + jnp.dot(part, band, preferred_element_type=jnp.float32)
        inv[...] = 1.0 / (jnp.sqrt(energy / PATCH + EPS) * math.sqrt(PATCH))
        dsum[...] = jnp.zeros_like(dsum)
        dmax[...] = jnp.full_like(dmax, -jnp.inf)

    c0 = pl.multiple_of(step * CB, CB)
    wide = CB + TC
    lane_w = lax.broadcasted_iota(jnp.int32, (wide, TL), 1)
    e0 = ext_ref[0, pl.ds(c0, wide), :]
    e1 = ext_ref[1, pl.ds(c0, wide), :]
    f1[...] = e1
    for a in range(nb):
        if a == 0:
            xa = e0
        else:
            sh = TL - W * a
            xa = jnp.where(lane_w < sh, pltpu.roll(e0, sh, 1), pltpu.roll(e1, sh, 1))
        hi = xa.astype(jnp.bfloat16).astype(jnp.float32)
        fhi[a] = hi
        flo[a] = xa - hi
    for a in range(nb):
        for i in range(TC):
            lhi[a * CB:(a + 1) * CB, i * TL:(i + 1) * TL] = fhi[a, i:i + CB, :].astype(jnp.bfloat16)
            llo[a * CB:(a + 1) * CB, i * TL:(i + 1) * TL] = flo[a, i:i + CB, :].astype(jnp.bfloat16)
    block = lax.broadcasted_iota(jnp.int32, (CB, TL), 1) // W
    for g in range(2):
        turned = []
        for p in range(8):
            y = f1[g * 8 + p:g * 8 + p + CB, :]
            turned.append(pltpu.roll(y, W * p, 1) if p else y)
        for a in range(nb):
            pick = turned[0]
            for p in range(1, 8):
                pick = jnp.where(block == (a + p) % 8, turned[p], pick)
            if a:
                pick = pltpu.roll(pick, TL - W * a, 1)
            hi, lo = split(pick)
            lhi[a * CB:(a + 1) * CB, HEADS + g * TL:HEADS + (g + 1) * TL] = hi
            llo[a * CB:(a + 1) * CB, HEADS + g * TL:HEADS + (g + 1) * TL] = lo

    def mm(x, y):
        return lax.dot_general(x, y, (((1,), (1,)), ((), ())), preferred_element_type=jnp.float32)

    acc[...] = mm(lhi[...], whi[...]) + mm(lhi[...], wlo[...]) + mm(llo[...], whi[...])

    scale = inv[pl.ds(c0, CB), :]
    for kg in range(count // 8):
        turned = []
        for a in range(nb):
            v = acc[a * CB:(a + 1) * CB, kg * TL:(kg + 1) * TL]
            turned.append(pltpu.roll(v, W * a, 1) if a else v)
        for q in range(8):
            pick = turned[0]
            for a in range(1, nb):
                pick = jnp.where(block == (q + a) % 8, turned[a], pick)
            if q:
                pick = pltpu.roll(pick, TL - W * q, 1)
            z = pick * scale
            k = kg * 8 + q
            z_ref[k] = z
            s = z[0:8]
            m = z[0:8]
            for r in range(8, CB, 8):
                s = s + z[r:r + 8]
                m = jnp.maximum(m, z[r:r + 8])
            dsum[k] = dsum[k] + s
            dmax[k] = jnp.maximum(dmax[k], m)

    @pl.when(step == pl.num_programs(0) - 1)
    def _():
        sum_ref[...] = jnp.sum(dsum[...], axis=1)
        max_ref[...] = jnp.max(dmax[...], axis=1)


def correlate(ext, templates):
    rows = ext.shape[1] - TC
    count = templates.shape[0]
    steps = rows // CB
    m = CB * TL // W
    return pl.pallas_call(
        correlate_kernel,
        grid=(steps,),
        out_shape=(
            jax.ShapeDtypeStruct((count, rows, TL), jnp.float32),
            jax.ShapeDtypeStruct((count, TL), jnp.float32),
            jax.ShapeDtypeStruct((count, TL), jnp.float32),
        ),
        in_specs=[
            pl.BlockSpec(ext.shape, lambda s: (0, 0, 0)),
            pl.BlockSpec(templates.shape, lambda s: (0, 0)),
        ],
        out_specs=(
            pl.BlockSpec((count, CB, TL), lambda s: (0, s, 0)),
            pl.BlockSpec((count, TL), lambda s: (0, 0)),
            pl.BlockSpec((count, TL), lambda s: (0, 0)),
        ),
        scratch_shapes=[
            pltpu.VMEM((count * W, DEPTH), jnp.bfloat16),
            pltpu.VMEM((count * W, DEPTH), jnp.bfloat16),
            pltpu.VMEM((m, DEPTH), jnp.bfloat16),
            pltpu.VMEM((m, DEPTH), jnp.bfloat16),
            pltpu.VMEM((count, PATCH), jnp.float32),
            pltpu.VMEM((rows, TL), jnp.float32),
            pltpu.VMEM((CB + TC, TL), jnp.float32),
            pltpu.VMEM((TL // W, CB + TC, TL), jnp.float32),
            pltpu.VMEM((TL // W, CB + TC, TL), jnp.float32),
            pltpu.VMEM((m, count * W), jnp.float32),
            pltpu.VMEM((count, 8, TL), jnp.float32),
            pltpu.VMEM((count, 8, TL), jnp.float32),
        ],
        compiler_params=pltpu.CompilerParams(vmem_limit_bytes=48 << 20),
    )(ext, templates)


def reduce_kernel(nc, half, x_ref, out_ref, slots, send, recv, send2, recv2):
    c = lax.axis_index("chan")
    t = lax.axis_index("tm")
    barrier = pltpu.get_barrier_semaphore()
    for d in range(1, nc):
        pl.semaphore_signal(barrier, inc=1, device_id=(lax.rem(c + d, nc), t), device_id_type=MESH)
    pl.semaphore_wait(barrier, nc - 1)
    first = []
    for d in range(1, nc):
        to = lax.rem(c + d, nc)
        cp = pltpu.make_async_remote_copy(
            src_ref=x_ref.at[to], dst_ref=slots.at[d],
            send_sem=send.at[d], recv_sem=recv.at[d],
            device_id=(to, t), device_id_type=MESH)
        cp.start()
        first.append(cp)
    total = x_ref[c]
    top = total
    for d in range(1, nc):
        first[d - 1].wait_recv()
        v = slots[d]
        total = total + v
        top = jnp.maximum(top, v)
    per = x_ref.shape[1]
    row = c * per + lax.broadcasted_iota(jnp.int32, total.shape, 0)
    out_ref[c] = jnp.where(row < half, total, top)
    second = []
    for d in range(1, nc):
        to = lax.rem(c + d, nc)
        cp = pltpu.make_async_remote_copy(
            src_ref=out_ref.at[c], dst_ref=out_ref.at[c],
            send_sem=send2.at[d], recv_sem=recv2.at[d],
            device_id=(to, t), device_id_type=MESH)
        cp.start()
        second.append(cp)
    for cp in first:
        cp.wait_send()
    for cp in second:
        cp.wait()


def reduce_all(x, nc, half):
    vmem = pl.BlockSpec(memory_space=pltpu.VMEM)
    sems = pltpu.SemaphoreType.DMA((nc,))
    return pl.pallas_call(
        functools.partial(reduce_kernel, nc, half),
        out_shape=jax.ShapeDtypeStruct(x.shape, jnp.float32),
        in_specs=[vmem],
        out_specs=vmem,
        scratch_shapes=[pltpu.VMEM(x.shape, jnp.float32), sems, sems, sems, sems],
        compiler_params=pltpu.CompilerParams(collective_id=1, has_side_effects=True),
    )(x)


def on_device(data, templates):
    nc = lax.axis_size("chan")
    nt = lax.axis_size("tm")
    rows = data.shape[0]
    ext, tall = exchange(data, templates, nc, nt)
    count = nt * templates.shape[0]
    zscore, sums, tops = correlate(ext, tall.reshape(count, PATCH))
    both = jnp.concatenate([sums, tops], axis=0).reshape(nc, 2 * count // nc, TL)
    both = reduce_all(both, nc, count).reshape(2 * count, TL)
    detection = both[:count] / math.sqrt(rows * nc)
    return (zscore, detection, both[count:])


def solution(mesh):
    placed = (P("chan", "tm"), P("tm", None))
    return jax.shard_map(
        on_device,
        mesh=mesh,
        in_specs=placed,
        out_specs=(P(None, "chan", "tm"), P(None, "tm"), P(None, "tm")),
        check_vma=False,
    )
```

```python
import functools
import math

import jax
import jax.numpy as jnp
from jax import lax
from jax.experimental import pallas as pl
from jax.experimental.pallas import tpu as pltpu
from jax.sharding import PartitionSpec as P

TC = 16
TL = 128
PATCH = 2048
EPS = 1e-06
W = 16
HEADS = TC * TL
DEPTH = HEADS + TC * W
CB = 32
MESH = pl.DeviceIdType.MESH


def exchange_kernel(nc, nt, data_ref, tmpl_ref, ext_ref, tall_ref, send, recv, tsend, trecv):
    rows = data_ref.shape[0]
    c = lax.axis_index("chan")
    t = lax.axis_index("tm")
    prev_t = lax.rem(t + nt - 1, nt)
    next_t = lax.rem(t + 1, nt)
    barrier = pltpu.get_barrier_semaphore()
    for d in range(1, nt):
        pl.semaphore_signal(barrier, inc=1, device_id=(c, lax.rem(t + d, nt)), device_id_type=MESH)

    @pl.when(c < nc - 1)
    def _():
        pl.semaphore_signal(barrier, inc=1, device_id=(c + 1, t), device_id_type=MESH)
        pl.semaphore_signal(barrier, inc=1, device_id=(c + 1, next_t), device_id_type=MESH)

    ext_ref[0, 0:rows, :] = data_ref[...]
    tall_ref[t] = tmpl_ref[...]

    @pl.when(c == nc - 1)
    def _():
        ext_ref[:, rows:, :] = jnp.zeros((2, TC, ext_ref.shape[2]), jnp.float32)

    @pl.when(c > 0)
    def _():
        pl.semaphore_wait(barrier, nt + 1)

    @pl.when(c == 0)
    def _():
        pl.semaphore_wait(barrier, nt - 1)

    def side(which, slot, device):
        return pltpu.make_async_remote_copy(
            src_ref=data_ref.at[pl.ds(0, TC)], dst_ref=ext_ref.at[which, pl.ds(rows, TC)],
            send_sem=send.at[slot], recv_sem=recv.at[slot],
            device_id=device, device_id_type=MESH)

    trail = pltpu.make_async_remote_copy(
        src_ref=data_ref, dst_ref=ext_ref.at[1, pl.ds(0, rows)],
        send_sem=send.at[0], recv_sem=recv.at[0],
        device_id=(c, prev_t), device_id_type=MESH)

    @pl.when(c > 0)
    def _():
        side(0, 1, (c - 1, t)).start()
        side(1, 2, (c - 1, prev_t)).start()

    every = []
    for d in range(1, nt):
        cp = pltpu.make_async_remote_copy(
            src_ref=tmpl_ref, dst_ref=tall_ref.at[t],
            send_sem=tsend.at[d - 1], recv_sem=trecv.at[d - 1],
            device_id=(c, lax.rem(t + d, nt)), device_id_type=MESH)
        cp.start()
        every.append(cp)
    trail.start()
    for cp in every:
        cp.wait()
    trail.wait()

    @pl.when(c > 0)
    def _():
        side(0, 1, (c - 1, t)).wait_send()
        side(1, 2, (c - 1, prev_t)).wait_send()

    @pl.when(c < nc - 1)
    def _():
        side(0, 1, (c, t)).wait_recv()
        side(1, 2, (c, t)).wait_recv()


def exchange(data, templates, nc, nt):
    rows, cols = data.shape
    kt = templates.shape[0]
    vmem = pl.BlockSpec(memory_space=pltpu.VMEM)
    return pl.pallas_call(
        functools.partial(exchange_kernel, nc, nt),
        out_shape=(
            jax.ShapeDtypeStruct((2, rows + TC, cols), jnp.float32),
            jax.ShapeDtypeStruct((nt, kt, PATCH), jnp.float32),
        ),
        in_specs=[vmem, vmem],
        out_specs=(vmem, vmem),
        scratch_shapes=[
            pltpu.SemaphoreType.DMA((3,)),
            pltpu.SemaphoreType.DMA((3,)),
            pltpu.SemaphoreType.DMA((max(nt - 1, 1),)),
            pltpu.SemaphoreType.DMA((max(nt - 1, 1),)),
        ],
        compiler_params=pltpu.CompilerParams(collective_id=0, has_side_effects=True),
    )(data, templates)


def split(x):
    hi = x.astype(jnp.bfloat16)
    lo = (x - hi.astype(jnp.float32)).astype(jnp.bfloat16)
    return hi, lo


def correlate_kernel(ext_ref, tmpl_ref, z_ref, sum_ref, max_ref,
                     whi, wlo, lhi, llo, w32, tn, inv, f1, fhi, flo, acc, dsum, dmax):
    step = pl.program_id(0)
    count = tmpl_ref.shape[0]
    rows = inv.shape[0]
    nb = TL // W

    @pl.when(step == 0)
    def _():
        tmpl = tmpl_ref[...]
        spread = jnp.sqrt(jnp.sum(tmpl * tmpl, axis=1, keepdims=True) / PATCH + EPS)
        tn[...] = tmpl * (1.0 / spread)

        lane8 = lax.broadcasted_iota(jnp.int32, (8, TL), 1)
        for kg in range(count // 8):
            rows8 = slice(kg * 8, kg * 8 + 8)
            ends = []
            for g in range(2):
                end = None
                for p in range(8):
                    i = g * 8 + p
                    t = tn[rows8, i * TL:(i + 1) * TL]
                    sh = (W * p + W) % TL
                    t = pltpu.roll(t, sh, 1) if sh else t
                    end = t if end is None else jnp.where(lane8 // W == p, t, end)
                ends.append(end)
            for b in range(W):
                spot = pl.ds(kg * 8 * W + b, 8, stride=W)
                for i in range(TC):
                    t = tn[rows8, i * TL:(i + 1) * TL]
                    if b:
                        t = jnp.where(lane8 >= b, pltpu.roll(t, b, 1), 0.0)
                    w32[i, spot, :] = t
                for g in range(2):
                    t = jnp.zeros((8, TL), jnp.float32)
                    if b:
                        t = jnp.where(lane8 % W < b, pltpu.roll(ends[g], TL - W + b, 1), 0.0)
                    w32[TC + g, spot, :] = t
        for j in range(DEPTH // TL):
            hi, lo = split(w32[j])
            whi[:, j * TL:(j + 1) * TL] = hi
            wlo[:, j * TL:(j + 1) * TL] = lo
        pieces = []
        for h in range(2):
            sq = ext_ref[h] * ext_ref[h]
            s = sq[0:rows + 8] + sq[1:rows + 9]
            s = s[0:rows + 6] + s[2:rows + 8]
            s = s[0:rows + 2] + s[4:rows + 6]
            e = sq[8:rows + TC]
            s_low = s[0:rows]
            u = e[0:rows + 7] + e[1:rows + 8]
            u = u[0:rows + 5] + u[2:rows + 7]
            u = u[0:rows] + u[4:rows + 4]
            pieces.append(s_low + u)
        win = jnp.concatenate(pieces, axis=1)
        src = lax.broadcasted_iota(jnp.int32, (2 * TL, TL), 0)
        dst = lax.broadcasted_iota(jnp.int32, (2 * TL, TL), 1)
        band = jnp.where((src >= dst) & (src < dst + TL), 1.0, 0.0).astype(jnp.bfloat16)
        energy = jnp.zeros((rows, TL), jnp.float32)
        rest = win
        for _ in range(3):
            part = rest.astype(jnp.bfloat16)
            rest = rest - part.astype(jnp.float32)
            energy = energy + jnp.dot(part, band, preferred_element_type=jnp.float32)
        inv[...] = 1.0 / (jnp.sqrt(energy / PATCH + EPS) * math.sqrt(PATCH))
        dsum[...] = jnp.zeros_like(dsum)
        dmax[...] = jnp.full_like(dmax, -jnp.inf)

    c0 = pl.multiple_of(step * CB, CB)
    wide = CB + TC
    lane_w = lax.broadcasted_iota(jnp.int32, (wide, TL), 1)
    e0 = ext_ref[0, pl.ds(c0, wide), :]
    e1 = ext_ref[1, pl.ds(c0, wide), :]
    f1[...] = e1
    for a in range(nb):
        if a == 0:
            xa = e0
        else:
            sh = TL - W * a
            xa = jnp.where(lane_w < sh, pltpu.roll(e0, sh, 1), pltpu.roll(e1, sh, 1))
        hi = xa.astype(jnp.bfloat16).astype(jnp.float32)
        fhi[a] = hi
        flo[a] = xa - hi
    for a in range(nb):
        for i in range(TC):
            lhi[a * CB:(a + 1) * CB, i * TL:(i + 1) * TL] = fhi[a, i:i + CB, :].astype(jnp.bfloat16)
            llo[a * CB:(a + 1) * CB, i * TL:(i + 1) * TL] = flo[a, i:i + CB, :].astype(jnp.bfloat16)
    block = lax.broadcasted_iota(jnp.int32, (CB, TL), 1) // W
    for g in range(2):
        turned = []
        for p in range(8):
            y = f1[g * 8 + p:g * 8 + p + CB, :]
            turned.append(pltpu.roll(y, W * p, 1) if p else y)
        for a in range(nb):
            pick = turned[0]
            for p in range(1, 8):
                pick = jnp.where(block == (a + p) % 8, turned[p], pick)
            if a:
                pick = pltpu.roll(pick, TL - W * a, 1)
            hi, lo = split(pick)
            lhi[a * CB:(a + 1) * CB, HEADS + g * TL:HEADS + (g + 1) * TL] = hi
            llo[a * CB:(a + 1) * CB, HEADS + g * TL:HEADS + (g + 1) * TL] = lo

    def mm(x, y):
        return lax.dot_general(x, y, (((1,), (1,)), ((), ())), preferred_element_type=jnp.float32)

    acc[...] = mm(lhi[...], whi[...]) + mm(lhi[...], wlo[...]) + mm(llo[...], whi[...])

    scale = inv[pl.ds(c0, CB), :]
    for kg in range(count // 8):
        turned = []
        for a in range(nb):
            v = acc[a * CB:(a + 1) * CB, kg * TL:(kg + 1) * TL]
            turned.append(pltpu.roll(v, W * a, 1) if a else v)
        for q in range(8):
            pick = turned[0]
            for a in range(1, nb):
                pick = jnp.where(block == (q + a) % 8, turned[a], pick)
            if q:
                pick = pltpu.roll(pick, TL - W * q, 1)
            z = pick * scale
            k = kg * 8 + q
            z_ref[k] = z
            s = z[0:8]
            m = z[0:8]
            for r in range(8, CB, 8):
                s = s + z[r:r + 8]
                m = jnp.maximum(m, z[r:r + 8])
            dsum[k] = dsum[k] + s
            dmax[k] = jnp.maximum(dmax[k], m)

    @pl.when(step == pl.num_programs(0) - 1)
    def _():
        sum_ref[...] = jnp.sum(dsum[...], axis=1)
        max_ref[...] = jnp.max(dmax[...], axis=1)


def correlate(ext, templates):
    rows = ext.shape[1] - TC
    count = templates.shape[0]
    steps = rows // CB
    m = CB * TL // W
    return pl.pallas_call(
        correlate_kernel,
        grid=(steps,),
        out_shape=(
            jax.ShapeDtypeStruct((count, rows, TL), jnp.float32),
            jax.ShapeDtypeStruct((count, TL), jnp.float32),
            jax.ShapeDtypeStruct((count, TL), jnp.float32),
        ),
        in_specs=[
            pl.BlockSpec(ext.shape, lambda s: (0, 0, 0)),
            pl.BlockSpec(templates.shape, lambda s: (0, 0)),
        ],
        out_specs=(
            pl.BlockSpec((count, CB, TL), lambda s: (0, s, 0)),
            pl.BlockSpec((count, TL), lambda s: (0, 0)),
            pl.BlockSpec((count, TL), lambda s: (0, 0)),
        ),
        scratch_shapes=[
            pltpu.VMEM((count * W, DEPTH), jnp.bfloat16),
            pltpu.VMEM((count * W, DEPTH), jnp.bfloat16),
            pltpu.VMEM((m, DEPTH), jnp.bfloat16),
            pltpu.VMEM((m, DEPTH), jnp.bfloat16),
            pltpu.VMEM((DEPTH // TL, count * W, TL), jnp.float32),
            pltpu.VMEM((count, PATCH), jnp.float32),
            pltpu.VMEM((rows, TL), jnp.float32),
            pltpu.VMEM((CB + TC, TL), jnp.float32),
            pltpu.VMEM((TL // W, CB + TC, TL), jnp.float32),
            pltpu.VMEM((TL // W, CB + TC, TL), jnp.float32),
            pltpu.VMEM((m, count * W), jnp.float32),
            pltpu.VMEM((count, 8, TL), jnp.float32),
            pltpu.VMEM((count, 8, TL), jnp.float32),
        ],
        compiler_params=pltpu.CompilerParams(vmem_limit_bytes=48 << 20),
    )(ext, templates)


def reduce_kernel(nc, half, x_ref, out_ref, slots, send, recv, send2, recv2):
    c = lax.axis_index("chan")
    t = lax.axis_index("tm")
    barrier = pltpu.get_barrier_semaphore()
    for d in range(1, nc):
        pl.semaphore_signal(barrier, inc=1, device_id=(lax.rem(c + d, nc), t), device_id_type=MESH)
    pl.semaphore_wait(barrier, nc - 1)
    first = []
    for d in range(1, nc):
        to = lax.rem(c + d, nc)
        cp = pltpu.make_async_remote_copy(
            src_ref=x_ref.at[to], dst_ref=slots.at[d],
            send_sem=send.at[d], recv_sem=recv.at[d],
            device_id=(to, t), device_id_type=MESH)
        cp.start()
        first.append(cp)
    total = x_ref[c]
    top = total
    for d in range(1, nc):
        first[d - 1].wait_recv()
        v = slots[d]
        total = total + v
        top = jnp.maximum(top, v)
    per = x_ref.shape[1]
    row = c * per + lax.broadcasted_iota(jnp.int32, total.shape, 0)
    out_ref[c] = jnp.where(row < half, total, top)
    second = []
    for d in range(1, nc):
        to = lax.rem(c + d, nc)
        cp = pltpu.make_async_remote_copy(
            src_ref=out_ref.at[c], dst_ref=out_ref.at[c],
            send_sem=send2.at[d], recv_sem=recv2.at[d],
            device_id=(to, t), device_id_type=MESH)
        cp.start()
        second.append(cp)
    for cp in first:
        cp.wait_send()
    for cp in second:
        cp.wait()


def reduce_all(x, nc, half):
    vmem = pl.BlockSpec(memory_space=pltpu.VMEM)
    sems = pltpu.SemaphoreType.DMA((nc,))
    return pl.pallas_call(
        functools.partial(reduce_kernel, nc, half),
        out_shape=jax.ShapeDtypeStruct(x.shape, jnp.float32),
        in_specs=[vmem],
        out_specs=vmem,
        scratch_shapes=[pltpu.VMEM(x.shape, jnp.float32), sems, sems, sems, sems],
        compiler_params=pltpu.CompilerParams(collective_id=1, has_side_effects=True),
    )(x)


def on_device(data, templates):
    nc = lax.axis_size("chan")
    nt = lax.axis_size("tm")
    rows = data.shape[0]
    ext, tall = exchange(data, templates, nc, nt)
    count = nt * templates.shape[0]
    zscore, sums, tops = correlate(ext, tall.reshape(count, PATCH))
    both = jnp.concatenate([sums, tops], axis=0).reshape(nc, 2 * count // nc, TL)
    both = reduce_all(both, nc, count).reshape(2 * count, TL)
    detection = both[:count] / math.sqrt(rows * nc)
    return (zscore, detection, both[count:])


def solution(mesh):
    placed = (P("chan", "tm"), P("tm", None))
    return jax.shard_map(
        on_device,
        mesh=mesh,
        in_specs=placed,
        out_specs=(P(None, "chan", "tm"), P(None, "tm"), P(None, "tm")),
        check_vma=False,
    )
```

```python
import functools
import math

import jax
import jax.numpy as jnp
from jax import lax
from jax.experimental import pallas as pl
from jax.experimental.pallas import tpu as pltpu
from jax.sharding import PartitionSpec as P

TC = 16
TL = 128
PATCH = 2048
EPS = 1e-06
W = 16
HEADS = TC * TL
DEPTH = HEADS + TC * W
CB = 32
MESH = pl.DeviceIdType.MESH


def exchange_kernel(nc, nt, data_ref, tmpl_ref, ext_ref, tall_ref, send, recv, tsend, trecv):
    rows = data_ref.shape[0]
    c = lax.axis_index("chan")
    t = lax.axis_index("tm")
    prev_t = lax.rem(t + nt - 1, nt)
    next_t = lax.rem(t + 1, nt)
    barrier = pltpu.get_barrier_semaphore()
    for d in range(1, nt):
        pl.semaphore_signal(barrier, inc=1, device_id=(c, lax.rem(t + d, nt)), device_id_type=MESH)

    @pl.when(c < nc - 1)
    def _():
        pl.semaphore_signal(barrier, inc=1, device_id=(c + 1, t), device_id_type=MESH)
        pl.semaphore_signal(barrier, inc=1, device_id=(c + 1, next_t), device_id_type=MESH)

    ext_ref[0, 0:rows, :] = data_ref[...]
    tall_ref[t] = tmpl_ref[...]

    @pl.when(c == nc - 1)
    def _():
        ext_ref[:, rows:, :] = jnp.zeros((2, TC, ext_ref.shape[2]), jnp.float32)

    @pl.when(c > 0)
    def _():
        pl.semaphore_wait(barrier, nt + 1)

    @pl.when(c == 0)
    def _():
        pl.semaphore_wait(barrier, nt - 1)

    def side(which, slot, device):
        return pltpu.make_async_remote_copy(
            src_ref=data_ref.at[pl.ds(0, TC)], dst_ref=ext_ref.at[which, pl.ds(rows, TC)],
            send_sem=send.at[slot], recv_sem=recv.at[slot],
            device_id=device, device_id_type=MESH)

    trail = pltpu.make_async_remote_copy(
        src_ref=data_ref, dst_ref=ext_ref.at[1, pl.ds(0, rows)],
        send_sem=send.at[0], recv_sem=recv.at[0],
        device_id=(c, prev_t), device_id_type=MESH)

    @pl.when(c > 0)
    def _():
        side(0, 1, (c - 1, t)).start()
        side(1, 2, (c - 1, prev_t)).start()

    every = []
    for d in range(1, nt):
        cp = pltpu.make_async_remote_copy(
            src_ref=tmpl_ref, dst_ref=tall_ref.at[t],
            send_sem=tsend.at[d - 1], recv_sem=trecv.at[d - 1],
            device_id=(c, lax.rem(t + d, nt)), device_id_type=MESH)
        cp.start()
        every.append(cp)
    trail.start()
    for cp in every:
        cp.wait()
    trail.wait()

    @pl.when(c > 0)
    def _():
        side(0, 1, (c - 1, t)).wait_send()
        side(1, 2, (c - 1, prev_t)).wait_send()

    @pl.when(c < nc - 1)
    def _():
        side(0, 1, (c, t)).wait_recv()
        side(1, 2, (c, t)).wait_recv()


def exchange(data, templates, nc, nt):
    rows, cols = data.shape
    kt = templates.shape[0]
    vmem = pl.BlockSpec(memory_space=pltpu.VMEM)
    return pl.pallas_call(
        functools.partial(exchange_kernel, nc, nt),
        out_shape=(
            jax.ShapeDtypeStruct((2, rows + TC, cols), jnp.float32),
            jax.ShapeDtypeStruct((nt, kt, PATCH), jnp.float32),
        ),
        in_specs=[vmem, vmem],
        out_specs=(vmem, vmem),
        scratch_shapes=[
            pltpu.SemaphoreType.DMA((3,)),
            pltpu.SemaphoreType.DMA((3,)),
            pltpu.SemaphoreType.DMA((max(nt - 1, 1),)),
            pltpu.SemaphoreType.DMA((max(nt - 1, 1),)),
        ],
        compiler_params=pltpu.CompilerParams(collective_id=0, has_side_effects=True),
    )(data, templates)


def split(x):
    hi = x.astype(jnp.bfloat16)
    lo = (x - hi.astype(jnp.float32)).astype(jnp.bfloat16)
    return hi, lo


def correlate_kernel(ext_hbm, tmpl_hbm, z_ref, both_ref, ext_ref, tmpl_ref, sems,
                     whi, wlo, lhi, llo, w32, tn, inv, f1, fhi, flo, acc, dsum, dmax):
    step = pl.program_id(0)
    count = tmpl_ref.shape[0]
    rows = inv.shape[0]
    nb = TL // W

    @pl.when(step == 0)
    def _():
        get_tmpl = pltpu.make_async_copy(tmpl_hbm, tmpl_ref, sems.at[0])
        get_ext = pltpu.make_async_copy(ext_hbm, ext_ref, sems.at[1])
        get_tmpl.start()
        get_ext.start()
        get_tmpl.wait()
        tmpl = tmpl_ref[...]
        spread = jnp.sqrt(jnp.sum(tmpl * tmpl, axis=1, keepdims=True) / PATCH + EPS)
        tn[...] = tmpl * (1.0 / spread)

        lane8 = lax.broadcasted_iota(jnp.int32, (8, TL), 1)
        for kg in range(count // 8):
            rows8 = slice(kg * 8, kg * 8 + 8)
            ends = []
            for g in range(2):
                end = None
                for p in range(8):
                    i = g * 8 + p
                    t = tn[rows8, i * TL:(i + 1) * TL]
                    sh = (W * p + W) % TL
                    t = pltpu.roll(t, sh, 1) if sh else t
                    end = t if end is None else jnp.where(lane8 // W == p, t, end)
                ends.append(end)
            for b in range(W):
                spot = pl.ds(kg * 8 * W + b, 8, stride=W)
                for i in range(TC):
                    t = tn[rows8, i * TL:(i + 1) * TL]
                    if b:
                        t = jnp.where(lane8 >= b, pltpu.roll(t, b, 1), 0.0)
                    w32[i, spot, :] = t
                for g in range(2):
                    t = jnp.zeros((8, TL), jnp.float32)
                    if b:
                        t = jnp.where(lane8 % W < b, pltpu.roll(ends[g], TL - W + b, 1), 0.0)
                    w32[TC + g, spot, :] = t
        for j in range(DEPTH // TL):
            hi, lo = split(w32[j])
            whi[:, j * TL:(j + 1) * TL] = hi
            wlo[:, j * TL:(j + 1) * TL] = lo
        get_ext.wait()
        pieces = []
        for h in range(2):
            sq = ext_ref[h] * ext_ref[h]
            s = sq[0:rows + 8] + sq[1:rows + 9]
            s = s[0:rows + 6] + s[2:rows + 8]
            s = s[0:rows + 2] + s[4:rows + 6]
            e = sq[8:rows + TC]
            s_low = s[0:rows]
            u = e[0:rows + 7] + e[1:rows + 8]
            u = u[0:rows + 5] + u[2:rows + 7]
            u = u[0:rows] + u[4:rows + 4]
            pieces.append(s_low + u)
        win = jnp.concatenate(pieces, axis=1)
        src = lax.broadcasted_iota(jnp.int32, (2 * TL, TL), 0)
        dst = lax.broadcasted_iota(jnp.int32, (2 * TL, TL), 1)
        band = jnp.where((src >= dst) & (src < dst + TL), 1.0, 0.0).astype(jnp.bfloat16)
        energy = jnp.zeros((rows, TL), jnp.float32)
        rest = win
        for _ in range(3):
            part = rest.astype(jnp.bfloat16)
            rest = rest - part.astype(jnp.float32)
            energy = energy + jnp.dot(part, band, preferred_element_type=jnp.float32)
        inv[...] = 1.0 / (jnp.sqrt(energy / PATCH + EPS) * math.sqrt(PATCH))
        dsum[...] = jnp.zeros_like(dsum)
        dmax[...] = jnp.full_like(dmax, -jnp.inf)

    c0 = pl.multiple_of(step * CB, CB)
    wide = CB + TC
    lane_w = lax.broadcasted_iota(jnp.int32, (wide, TL), 1)
    e0 = ext_ref[0, pl.ds(c0, wide), :]
    e1 = ext_ref[1, pl.ds(c0, wide), :]
    f1[...] = e1
    for a in range(nb):
        if a == 0:
            xa = e0
        else:
            sh = TL - W * a
            xa = jnp.where(lane_w < sh, pltpu.roll(e0, sh, 1), pltpu.roll(e1, sh, 1))
        hi = xa.astype(jnp.bfloat16).astype(jnp.float32)
        fhi[a] = hi
        flo[a] = xa - hi
    for a in range(nb):
        for i in range(TC):
            lhi[a * CB:(a + 1) * CB, i * TL:(i + 1) * TL] = fhi[a, i:i + CB, :].astype(jnp.bfloat16)
            llo[a * CB:(a + 1) * CB, i * TL:(i + 1) * TL] = flo[a, i:i + CB, :].astype(jnp.bfloat16)
    block = lax.broadcasted_iota(jnp.int32, (CB, TL), 1) // W
    for g in range(2):
        turned = []
        for p in range(8):
            y = f1[g * 8 + p:g * 8 + p + CB, :]
            turned.append(pltpu.roll(y, W * p, 1) if p else y)
        for a in range(nb):
            pick = turned[0]
            for p in range(1, 8):
                pick = jnp.where(block == (a + p) % 8, turned[p], pick)
            if a:
                pick = pltpu.roll(pick, TL - W * a, 1)
            hi, lo = split(pick)
            lhi[a * CB:(a + 1) * CB, HEADS + g * TL:HEADS + (g + 1) * TL] = hi
            llo[a * CB:(a + 1) * CB, HEADS + g * TL:HEADS + (g + 1) * TL] = lo

    def mm(x, y):
        return lax.dot_general(x, y, (((1,), (1,)), ((), ())), preferred_element_type=jnp.float32)

    acc[...] = mm(lhi[...], whi[...]) + mm(lhi[...], wlo[...]) + mm(llo[...], whi[...])

    scale = inv[pl.ds(c0, CB), :]
    for kg in range(count // 8):
        turned = []
        for a in range(nb):
            v = acc[a * CB:(a + 1) * CB, kg * TL:(kg + 1) * TL]
            turned.append(pltpu.roll(v, W * a, 1) if a else v)
        for q in range(8):
            pick = turned[0]
            for a in range(1, nb):
                pick = jnp.where(block == (q + a) % 8, turned[a], pick)
            if q:
                pick = pltpu.roll(pick, TL - W * q, 1)
            z = pick * scale
            k = kg * 8 + q
            z_ref[k] = z
            s = z[0:8]
            m = z[0:8]
            for r in range(8, CB, 8):
                s = s + z[r:r + 8]
                m = jnp.maximum(m, z[r:r + 8])
            dsum[k] = dsum[k] + s
            dmax[k] = jnp.maximum(dmax[k], m)

    @pl.when(step == pl.num_programs(0) - 1)
    def _():
        both_ref[0:count] = jnp.sum(dsum[...], axis=1)
        both_ref[count:] = jnp.max(dmax[...], axis=1)


def correlate(ext, templates):
    rows = ext.shape[1] - TC
    count = templates.shape[0]
    steps = rows // CB
    m = CB * TL // W
    return pl.pallas_call(
        correlate_kernel,
        grid=(steps,),
        out_shape=(
            jax.ShapeDtypeStruct((count, rows, TL), jnp.float32),
            jax.ShapeDtypeStruct((2 * count, TL), jnp.float32),
        ),
        in_specs=[
            pl.BlockSpec(memory_space=pl.ANY),
            pl.BlockSpec(memory_space=pl.ANY),
        ],
        out_specs=(
            pl.BlockSpec((count, CB, TL), lambda s: (0, s, 0)),
            pl.BlockSpec((2 * count, TL), lambda s: (0, 0)),
        ),
        scratch_shapes=[
            pltpu.VMEM(ext.shape, jnp.float32),
            pltpu.VMEM(templates.shape, jnp.float32),
            pltpu.SemaphoreType.DMA((2,)),
            pltpu.VMEM((count * W, DEPTH), jnp.bfloat16),
            pltpu.VMEM((count * W, DEPTH), jnp.bfloat16),
            pltpu.VMEM((m, DEPTH), jnp.bfloat16),
            pltpu.VMEM((m, DEPTH), jnp.bfloat16),
            pltpu.VMEM((DEPTH // TL, count * W, TL), jnp.float32),
            pltpu.VMEM((count, PATCH), jnp.float32),
            pltpu.VMEM((rows, TL), jnp.float32),
            pltpu.VMEM((CB + TC, TL), jnp.float32),
            pltpu.VMEM((TL // W, CB + TC, TL), jnp.float32),
            pltpu.VMEM((TL // W, CB + TC, TL), jnp.float32),
            pltpu.VMEM((m, count * W), jnp.float32),
            pltpu.VMEM((count, 8, TL), jnp.float32),
            pltpu.VMEM((count, 8, TL), jnp.float32),
        ],
        compiler_params=pltpu.CompilerParams(vmem_limit_bytes=60 << 20),
    )(ext, templates)


def reduce_kernel(nc, inner, root, x_ref, det_ref, peak_ref, slots1, slots2, full,
                  send1, recv1, send2, recv2, send3, recv3):
    c = lax.axis_index("chan")
    t = lax.axis_index("tm")
    outer = nc // inner
    o = c // inner
    q = c - o * inner
    part = slots1.shape[1]
    half = full.shape[0] // 2

    def near(d):
        return o * inner + lax.rem(q + d, inner)

    def far(d):
        return lax.rem(o + d, outer) * inner + q

    barrier = pltpu.get_barrier_semaphore()
    for d in range(1, inner):
        pl.semaphore_signal(barrier, inc=1, device_id=(near(d), t), device_id_type=MESH)
    for d in range(1, outer):
        pl.semaphore_signal(barrier, inc=1, device_id=(far(d), t), device_id_type=MESH)
    pl.semaphore_wait(barrier, inner + outer - 2)

    def mine(i):
        return pl.ds(pl.multiple_of(i * part, part), part)

    def join(x, y):
        return jnp.where(is_sum, x + y, jnp.maximum(x, y))

    is_sum = (q * part + lax.broadcasted_iota(jnp.int32, (part, x_ref.shape[1]), 0)) < half
    first = []
    for d in range(1, inner):
        to = near(d)
        cp = pltpu.make_async_remote_copy(
            src_ref=x_ref.at[mine(to - o * inner)], dst_ref=slots1.at[d],
            send_sem=send1.at[d], recv_sem=recv1.at[d],
            device_id=(to, t), device_id_type=MESH)
        cp.start()
        first.append(cp)
    total = x_ref[mine(q), :]
    for d in range(1, inner):
        first[d - 1].wait_recv()
        total = join(total, slots1[d])
    slots2[0] = total
    second = []
    for d in range(1, outer):
        cp = pltpu.make_async_remote_copy(
            src_ref=slots2.at[0], dst_ref=slots2.at[d],
            send_sem=send2.at[d], recv_sem=recv2.at[d],
            device_id=(far(d), t), device_id_type=MESH)
        cp.start()
        second.append(cp)
    for cp in second:
        cp.wait_recv()
    total = None
    for g in range(outer):
        v = slots2[lax.rem(o - g + outer, outer)]
        total = v if total is None else join(total, v)
    full[mine(q), :] = total
    third = []
    for d in range(1, inner):
        cp = pltpu.make_async_remote_copy(
            src_ref=full.at[mine(q)], dst_ref=full.at[mine(q)],
            send_sem=send3.at[d], recv_sem=recv3.at[d],
            device_id=(near(d), t), device_id_type=MESH)
        cp.start()
        third.append(cp)
    for cp in first + second:
        cp.wait_send()
    for cp in third:
        cp.wait()
    det_ref[...] = full[0:half] / root
    peak_ref[...] = full[half:]


def reduce_all(x, nc, total_chan):
    inner = 4 if nc % 4 == 0 else 1
    part = x.shape[0] // inner
    cols = x.shape[1]
    out = jax.ShapeDtypeStruct((x.shape[0] // 2, cols), jnp.float32)
    vmem = pl.BlockSpec(memory_space=pltpu.VMEM)
    near = pltpu.SemaphoreType.DMA((inner,))
    far = pltpu.SemaphoreType.DMA((nc // inner,))
    return pl.pallas_call(
        functools.partial(reduce_kernel, nc, inner, math.sqrt(total_chan)),
        out_shape=(out, out),
        in_specs=[vmem],
        out_specs=(vmem, vmem),
        scratch_shapes=[
            pltpu.VMEM((inner, part, cols), jnp.float32),
            pltpu.VMEM((nc // inner, part, cols), jnp.float32),
            pltpu.VMEM(x.shape, jnp.float32),
            near, near, far, far, near, near,
        ],
        compiler_params=pltpu.CompilerParams(collective_id=1, has_side_effects=True),
    )(x)


def on_device(data, templates):
    nc = lax.axis_size("chan")
    nt = lax.axis_size("tm")
    rows = data.shape[0]
    ext, tall = exchange(data, templates, nc, nt)
    zscore, both = correlate(ext, tall.reshape(nt * templates.shape[0], PATCH))
    detection, peak = reduce_all(both, nc, rows * nc)
    return (zscore, detection, peak)


def solution(mesh):
    placed = (P("chan", "tm"), P("tm", None))
    return jax.shard_map(
        on_device,
        mesh=mesh,
        in_specs=placed,
        out_specs=(P(None, "chan", "tm"), P(None, "tm"), P(None, "tm")),
        check_vma=False,
    )
```

```python
import functools
import math

import jax
import jax.numpy as jnp
from jax import lax
from jax.experimental import pallas as pl
from jax.experimental.pallas import tpu as pltpu
from jax.sharding import PartitionSpec as P

TC = 16
TL = 128
PATCH = 2048
EPS = 1e-06
W = 16
HEADS = TC * TL
DEPTH = HEADS + TC * W
CB = 32
MESH = pl.DeviceIdType.MESH


def exchange_kernel(nc, nt, data_ref, tmpl_ref, ext_ref, tall_ref, send, recv, tsend, trecv):
    rows = data_ref.shape[0]
    c = lax.axis_index("chan")
    t = lax.axis_index("tm")
    prev_t = lax.rem(t + nt - 1, nt)
    next_t = lax.rem(t + 1, nt)
    barrier = pltpu.get_barrier_semaphore()
    for d in range(1, nt):
        pl.semaphore_signal(barrier, inc=1, device_id=(c, lax.rem(t + d, nt)), device_id_type=MESH)

    @pl.when(c < nc - 1)
    def _():
        pl.semaphore_signal(barrier, inc=1, device_id=(c + 1, t), device_id_type=MESH)
        pl.semaphore_signal(barrier, inc=1, device_id=(c + 1, next_t), device_id_type=MESH)

    ext_ref[0, 0:rows, :] = data_ref[...]
    tall_ref[t] = tmpl_ref[...]

    @pl.when(c == nc - 1)
    def _():
        ext_ref[:, rows:, :] = jnp.zeros((2, TC, ext_ref.shape[2]), jnp.float32)

    @pl.when(c > 0)
    def _():
        pl.semaphore_wait(barrier, nt + 1)

    @pl.when(c == 0)
    def _():
        pl.semaphore_wait(barrier, nt - 1)

    def side(which, slot, device):
        return pltpu.make_async_remote_copy(
            src_ref=data_ref.at[pl.ds(0, TC)], dst_ref=ext_ref.at[which, pl.ds(rows, TC)],
            send_sem=send.at[slot], recv_sem=recv.at[slot],
            device_id=device, device_id_type=MESH)

    trail = pltpu.make_async_remote_copy(
        src_ref=data_ref, dst_ref=ext_ref.at[1, pl.ds(0, rows)],
        send_sem=send.at[0], recv_sem=recv.at[0],
        device_id=(c, prev_t), device_id_type=MESH)

    @pl.when(c > 0)
    def _():
        side(0, 1, (c - 1, t)).start()
        side(1, 2, (c - 1, prev_t)).start()

    every = []
    for d in range(1, nt):
        cp = pltpu.make_async_remote_copy(
            src_ref=tmpl_ref, dst_ref=tall_ref.at[t],
            send_sem=tsend.at[d - 1], recv_sem=trecv.at[d - 1],
            device_id=(c, lax.rem(t + d, nt)), device_id_type=MESH)
        cp.start()
        every.append(cp)
    trail.start()
    for cp in every:
        cp.wait()
    trail.wait()

    @pl.when(c > 0)
    def _():
        side(0, 1, (c - 1, t)).wait_send()
        side(1, 2, (c - 1, prev_t)).wait_send()

    @pl.when(c < nc - 1)
    def _():
        side(0, 1, (c, t)).wait_recv()
        side(1, 2, (c, t)).wait_recv()


def exchange(data, templates, nc, nt):
    rows, cols = data.shape
    kt = templates.shape[0]
    vmem = pl.BlockSpec(memory_space=pltpu.VMEM)
    return pl.pallas_call(
        functools.partial(exchange_kernel, nc, nt),
        out_shape=(
            jax.ShapeDtypeStruct((2, rows + TC, cols), jnp.float32),
            jax.ShapeDtypeStruct((nt, kt, PATCH), jnp.float32),
        ),
        in_specs=[vmem, vmem],
        out_specs=(vmem, vmem),
        scratch_shapes=[
            pltpu.SemaphoreType.DMA((3,)),
            pltpu.SemaphoreType.DMA((3,)),
            pltpu.SemaphoreType.DMA((max(nt - 1, 1),)),
            pltpu.SemaphoreType.DMA((max(nt - 1, 1),)),
        ],
        compiler_params=pltpu.CompilerParams(collective_id=0, has_side_effects=True),
    )(data, templates)


def split(x):
    hi = x.astype(jnp.bfloat16)
    lo = (x - hi.astype(jnp.float32)).astype(jnp.bfloat16)
    return hi, lo


def correlate_kernel(ext_hbm, tmpl_hbm, z_ref, both_ref, ext_ref, tmpl_ref, sems,
                     whi, wlo, lhi0, llo0, lhi1, llo1, w32, tn, inv, f1, fhi, flo,
                     acc0, acc1, dsum, dmax, zv, zsems):
    lhis, llos, accs = (lhi0, lhi1), (llo0, llo1), (acc0, acc1)
    count = tmpl_ref.shape[0]
    rows = inv.shape[0]
    nb = TL // W

    get_tmpl = pltpu.make_async_copy(tmpl_hbm, tmpl_ref, sems.at[0])
    get_ext = pltpu.make_async_copy(ext_hbm, ext_ref, sems.at[1])
    get_tmpl.start()
    get_ext.start()
    get_tmpl.wait()
    tmpl = tmpl_ref[...]
    spread = jnp.sqrt(jnp.sum(tmpl * tmpl, axis=1, keepdims=True) / PATCH + EPS)
    tn[...] = tmpl * (1.0 / spread)

    lane8 = lax.broadcasted_iota(jnp.int32, (8, TL), 1)
    for kg in range(count // 8):
        rows8 = slice(kg * 8, kg * 8 + 8)
        ends = []
        for g in range(2):
            end = None
            for p in range(8):
                i = g * 8 + p
                t = tn[rows8, i * TL:(i + 1) * TL]
                sh = (W * p + W) % TL
                t = pltpu.roll(t, sh, 1) if sh else t
                end = t if end is None else jnp.where(lane8 // W == p, t, end)
            ends.append(end)
        for b in range(W):
            spot = pl.ds(kg * 8 * W + b, 8, stride=W)
            for i in range(TC):
                t = tn[rows8, i * TL:(i + 1) * TL]
                if b:
                    t = jnp.where(lane8 >= b, pltpu.roll(t, b, 1), 0.0)
                w32[i, spot, :] = t
            for g in range(2):
                t = jnp.zeros((8, TL), jnp.float32)
                if b:
                    t = jnp.where(lane8 % W < b, pltpu.roll(ends[g], TL - W + b, 1), 0.0)
                w32[TC + g, spot, :] = t
    for j in range(DEPTH // TL):
        hi, lo = split(w32[j])
        whi[:, j * TL:(j + 1) * TL] = hi
        wlo[:, j * TL:(j + 1) * TL] = lo
    get_ext.wait()
    pieces = []
    for h in range(2):
        sq = ext_ref[h] * ext_ref[h]
        s = sq[0:rows + 8] + sq[1:rows + 9]
        s = s[0:rows + 6] + s[2:rows + 8]
        s = s[0:rows + 2] + s[4:rows + 6]
        e = sq[8:rows + TC]
        s_low = s[0:rows]
        u = e[0:rows + 7] + e[1:rows + 8]
        u = u[0:rows + 5] + u[2:rows + 7]
        u = u[0:rows] + u[4:rows + 4]
        pieces.append(s_low + u)
    win = jnp.concatenate(pieces, axis=1)
    src = lax.broadcasted_iota(jnp.int32, (2 * TL, TL), 0)
    dst = lax.broadcasted_iota(jnp.int32, (2 * TL, TL), 1)
    band = jnp.where((src >= dst) & (src < dst + TL), 1.0, 0.0).astype(jnp.bfloat16)
    energy = jnp.zeros((rows, TL), jnp.float32)
    rest = win
    for _ in range(3):
        part = rest.astype(jnp.bfloat16)
        rest = rest - part.astype(jnp.float32)
        energy = energy + jnp.dot(part, band, preferred_element_type=jnp.float32)
    inv[...] = 1.0 / (jnp.sqrt(energy / PATCH + EPS) * math.sqrt(PATCH))
    dsum[...] = jnp.zeros_like(dsum)
    dmax[...] = jnp.full_like(dmax, -jnp.inf)

    def mm(x, y):
        return lax.dot_general(x, y, (((1,), (1,)), ((), ())), preferred_element_type=jnp.float32)

    def prepare(c0, lhi, llo):
        wide = CB + TC
        lane_w = lax.broadcasted_iota(jnp.int32, (wide, TL), 1)
        e0 = ext_ref[0, c0:c0 + wide, :]
        e1 = ext_ref[1, c0:c0 + wide, :]
        f1[...] = e1
        for a in range(nb):
            if a == 0:
                xa = e0
            else:
                sh = TL - W * a
                xa = jnp.where(lane_w < sh, pltpu.roll(e0, sh, 1), pltpu.roll(e1, sh, 1))
            hi = xa.astype(jnp.bfloat16).astype(jnp.float32)
            fhi[a] = hi
            flo[a] = xa - hi
        for a in range(nb):
            for i in range(TC):
                lhi[a * CB:(a + 1) * CB, i * TL:(i + 1) * TL] = fhi[a, i:i + CB, :].astype(jnp.bfloat16)
                llo[a * CB:(a + 1) * CB, i * TL:(i + 1) * TL] = flo[a, i:i + CB, :].astype(jnp.bfloat16)
        block = lax.broadcasted_iota(jnp.int32, (CB, TL), 1) // W
        for g in range(2):
            turned = []
            for p in range(8):
                y = f1[g * 8 + p:g * 8 + p + CB, :]
                turned.append(pltpu.roll(y, W * p, 1) if p else y)
            for a in range(nb):
                pick = turned[0]
                for p in range(1, 8):
                    pick = jnp.where(block == (a + p) % 8, turned[p], pick)
                if a:
                    pick = pltpu.roll(pick, TL - W * a, 1)
                hi, lo = split(pick)
                lhi[a * CB:(a + 1) * CB, HEADS + g * TL:HEADS + (g + 1) * TL] = hi
                llo[a * CB:(a + 1) * CB, HEADS + g * TL:HEADS + (g + 1) * TL] = lo


    def multiply(lhi, llo, acc):
        acc[...] = mm(lhi[...], whi[...]) + mm(lhi[...], wlo[...]) + mm(llo[...], whi[...])

    def finish(c0, acc):
        block = lax.broadcasted_iota(jnp.int32, (CB, TL), 1) // W
        scale = inv[c0:c0 + CB, :]
        for kg in range(count // 8):
            turned = []
            for a in range(nb):
                v = acc[a * CB:(a + 1) * CB, kg * TL:(kg + 1) * TL]
                turned.append(pltpu.roll(v, W * a, 1) if a else v)
            for q in range(8):
                pick = turned[0]
                for a in range(1, nb):
                    pick = jnp.where(block == (q + a) % 8, turned[a], pick)
                if q:
                    pick = pltpu.roll(pick, TL - W * q, 1)
                z = pick * scale
                k = kg * 8 + q
                zv[k, c0:c0 + CB, :] = z
                s = z[0:8]
                m = z[0:8]
                for r in range(8, CB, 8):
                    s = s + z[r:r + 8]
                    m = jnp.maximum(m, z[r:r + 8])
                dsum[k] = dsum[k] + s
                dmax[k] = jnp.maximum(dmax[k], m)


    def ship(n):
        part = pl.ds(n * CB, CB)
        return pltpu.make_async_copy(zv.at[:, part], z_ref.at[:, part], zsems.at[n])

    steps = rows // CB
    prepare(0, lhis[0], llos[0])
    for n in range(steps):
        if n:
            finish((n - 1) * CB, accs[(n - 1) % 2])
        if n + 1 < steps:
            prepare((n + 1) * CB, lhis[(n + 1) % 2], llos[(n + 1) % 2])
        multiply(lhis[n % 2], llos[n % 2], accs[n % 2])
        if n:
            ship(n - 1).start()
    finish((steps - 1) * CB, accs[(steps - 1) % 2])
    ship(steps - 1).start()
    both_ref[0:count] = jnp.sum(dsum[...], axis=1)
    both_ref[count:] = jnp.max(dmax[...], axis=1)
    for n in range(steps):
        ship(n).wait()


def correlate(ext, templates):
    rows = ext.shape[1] - TC
    count = templates.shape[0]
    m = CB * TL // W
    return pl.pallas_call(
        correlate_kernel,
        out_shape=(
            jax.ShapeDtypeStruct((count, rows, TL), jnp.float32),
            jax.ShapeDtypeStruct((2 * count, TL), jnp.float32),
        ),
        in_specs=[
            pl.BlockSpec(memory_space=pl.ANY),
            pl.BlockSpec(memory_space=pl.ANY),
        ],
        out_specs=(
            pl.BlockSpec(memory_space=pl.ANY),
            pl.BlockSpec(memory_space=pltpu.VMEM),
        ),
        scratch_shapes=[
            pltpu.VMEM(ext.shape, jnp.float32),
            pltpu.VMEM(templates.shape, jnp.float32),
            pltpu.SemaphoreType.DMA((2,)),
            pltpu.VMEM((count * W, DEPTH), jnp.bfloat16),
            pltpu.VMEM((count * W, DEPTH), jnp.bfloat16),
            pltpu.VMEM((m, DEPTH), jnp.bfloat16),
            pltpu.VMEM((m, DEPTH), jnp.bfloat16),
            pltpu.VMEM((m, DEPTH), jnp.bfloat16),
            pltpu.VMEM((m, DEPTH), jnp.bfloat16),
            pltpu.VMEM((DEPTH // TL, count * W, TL), jnp.float32),
            pltpu.VMEM((count, PATCH), jnp.float32),
            pltpu.VMEM((rows, TL), jnp.float32),
            pltpu.VMEM((CB + TC, TL), jnp.float32),
            pltpu.VMEM((TL // W, CB + TC, TL), jnp.float32),
            pltpu.VMEM((TL // W, CB + TC, TL), jnp.float32),
            pltpu.VMEM((m, count * W), jnp.float32),
            pltpu.VMEM((m, count * W), jnp.float32),
            pltpu.VMEM((count, 8, TL), jnp.float32),
            pltpu.VMEM((count, 8, TL), jnp.float32),
            pltpu.VMEM((count, rows, TL), jnp.float32),
            pltpu.SemaphoreType.DMA((rows // CB,)),
        ],
        compiler_params=pltpu.CompilerParams(vmem_limit_bytes=60 << 20),
    )(ext, templates)


def reduce_kernel(nc, inner, x_ref, full, slots1, slots2,
                  send1, recv1, send2, recv2, send3, recv3):
    c = lax.axis_index("chan")
    t = lax.axis_index("tm")
    outer = nc // inner
    o = c // inner
    q = c - o * inner
    part = slots1.shape[1]
    half = full.shape[0] // 2

    def near(d):
        return o * inner + lax.rem(q + d, inner)

    def far(d):
        return lax.rem(o + d, outer) * inner + q

    barrier = pltpu.get_barrier_semaphore()
    for d in range(1, inner):
        pl.semaphore_signal(barrier, inc=1, device_id=(near(d), t), device_id_type=MESH)
    for d in range(1, outer):
        pl.semaphore_signal(barrier, inc=1, device_id=(far(d), t), device_id_type=MESH)
    pl.semaphore_wait(barrier, inner + outer - 2)

    def mine(i):
        return pl.ds(pl.multiple_of(i * part, part), part)

    def join(x, y):
        return jnp.where(is_sum, x + y, jnp.maximum(x, y))

    is_sum = (q * part + lax.broadcasted_iota(jnp.int32, (part, x_ref.shape[1]), 0)) < half
    first = []
    for d in range(1, inner):
        to = near(d)
        cp = pltpu.make_async_remote_copy(
            src_ref=x_ref.at[mine(to - o * inner)], dst_ref=slots1.at[d],
            send_sem=send1.at[d], recv_sem=recv1.at[d],
            device_id=(to, t), device_id_type=MESH)
        cp.start()
        first.append(cp)
    total = x_ref[mine(q), :]
    for d in range(1, inner):
        first[d - 1].wait_recv()
        total = join(total, slots1[d])
    slots2[0] = total
    second = []
    for d in range(1, outer):
        cp = pltpu.make_async_remote_copy(
            src_ref=slots2.at[0], dst_ref=slots2.at[d],
            send_sem=send2.at[d], recv_sem=recv2.at[d],
            device_id=(far(d), t), device_id_type=MESH)
        cp.start()
        second.append(cp)
    for cp in second:
        cp.wait_recv()
    total = None
    for g in range(outer):
        v = slots2[lax.rem(o - g + outer, outer)]
        total = v if total is None else join(total, v)
    full[mine(q), :] = total
    third = []
    for d in range(1, inner):
        cp = pltpu.make_async_remote_copy(
            src_ref=full.at[mine(q)], dst_ref=full.at[mine(q)],
            send_sem=send3.at[d], recv_sem=recv3.at[d],
            device_id=(near(d), t), device_id_type=MESH)
        cp.start()
        third.append(cp)
    for cp in first + second:
        cp.wait_send()
    for cp in third:
        cp.wait()


def reduce_all(x, nc):
    inner = 4 if nc % 4 == 0 else 1
    part = x.shape[0] // inner
    cols = x.shape[1]
    vmem = pl.BlockSpec(memory_space=pltpu.VMEM)
    near = pltpu.SemaphoreType.DMA((inner,))
    far = pltpu.SemaphoreType.DMA((nc // inner,))
    return pl.pallas_call(
        functools.partial(reduce_kernel, nc, inner),
        out_shape=jax.ShapeDtypeStruct(x.shape, jnp.float32),
        in_specs=[vmem],
        out_specs=vmem,
        scratch_shapes=[
            pltpu.VMEM((inner, part, cols), jnp.float32),
            pltpu.VMEM((nc // inner, part, cols), jnp.float32),
            near, near, far, far, near, near,
        ],
        compiler_params=pltpu.CompilerParams(collective_id=1, has_side_effects=True),
    )(x)


def on_device(data, templates):
    nc = lax.axis_size("chan")
    nt = lax.axis_size("tm")
    rows = data.shape[0]
    ext, tall = exchange(data, templates, nc, nt)
    zscore, both = correlate(ext, tall.reshape(nt * templates.shape[0], PATCH))
    both = reduce_all(both, nc)
    count = both.shape[0] // 2
    return (zscore, both[:count] / math.sqrt(rows * nc), both[count:])


def solution(mesh):
    placed = (P("chan", "tm"), P("tm", None))
    return jax.shard_map(
        on_device,
        mesh=mesh,
        in_specs=placed,
        out_specs=(P(None, "chan", "tm"), P(None, "tm"), P(None, "tm")),
        check_vma=False,
    )
```
